512 devices in a mesh: up: 32 (over z, x_hi, core), down: 16 (over x_lo, y).
Axes of the slice: x: 4 (x_hi: 2, x_lo: 2; x = x_hi * 2 + x_lo), y: 8, z: 8, core: 2. Of those that a mesh axis runs over, the one named last changes fastest.
Arguments:
- deltas: bfloat16 [256, 16384], P('down', 'up'), may hold values from -6 to 6
- gradients: bfloat16 [256, 16384], P('up', 'down'), may hold values from -0.375 to 0.375
- up_blocks: int32 [8, 64], P(None, 'up'), may hold values from 0 to 3, as said below
- down_blocks: int32 [64], P('down'), may hold values from 0 to 7, as said below
- decoder: bfloat16 [16384, 4608], P('up', 'down'), may hold values from -0.09375 to 0.09375
- encoder: bfloat16 [4608, 16384], P('up', 'down'), may hold values from -6 to 6
Outputs:
- edge_scores: float32 [16384, 16384], P('up', 'down')
The draws below stay inside these ranges and needn't reach their ends.
Inputs may be any that keep to these rules, and one draw needn't show every extreme that they name: `up_blocks`: for each window and each index i of up, the 2 entries in columns i * 2 to (i + 1) * 2 - 1 are distinct. `down_blocks`: for each index j of down, the 4 entries j * 4 to (j + 1) * 4 - 1 are distinct.
All inputs are finite; a program needn't handle non-finite values.
Results may differ from the reference program's by a relative error of at most 0.0003.
Values may be sent and summed in bfloat16 or wider, within the bound.
No kernel may reach another device: no remote copies, remote signals or barrier semaphores. Data moves between devices by JAX's collectives and lax.ppermute only.
A program may use at most 64 MiB of HBM per device.

```python
import jax
import jax.numpy as jnp
from jax import lax

D = 4608
VF_DEV = 1024
BLOCK = 128
UACT = 2
DACT = 4
WIN = 32
TOKENS = 256
WINDOWS = 8
UB_DEV = 4
VB_DEV = 8
UF = 16384
VF = 16384
N_UP = 32
N_DOWN = 16


def draw_up_blocks(key, part):
    ranked = jax.random.randint(key, (WINDOWS, N_UP, UB_DEV), 0, 1 << 20, dtype=jnp.int32)
    ranked = ranked * UB_DEV + jnp.arange(UB_DEV, dtype=jnp.int32)
    ordering = jnp.argsort(ranked, axis=-1, stable=True)
    return ordering[:, :, :UACT].reshape(WINDOWS, N_UP * UACT).astype(jnp.int32)


def draw_down_blocks(key, part):
    ranked = jax.random.randint(jax.random.fold_in(key, 7), (N_DOWN, VB_DEV), 0, 1 << 20, dtype=jnp.int32)
    ranked = ranked * VB_DEV + jnp.arange(VB_DEV, dtype=jnp.int32)
    ordering = jnp.argsort(ranked, axis=-1, stable=True)
    return ordering[:, :DACT].reshape(N_DOWN * DACT).astype(jnp.int32)


def level_of(key, shape, cuts, low, high):
    gain, own = 1.0, jax.random.fold_in(key, 6)
    for position, blocks in cuts:
        heights = jnp.exp(jax.random.uniform(jax.random.fold_in(own, position), (blocks,), jnp.float32, low / len(cuts), high / len(cuts)))
        gain = gain * jnp.repeat(heights, shape[position] // blocks).reshape([-1 if axis == position else 1 for axis in range(len(shape))])
    return gain


def normal_values(key, dims, scale, bound, split=(), kind=jnp.bfloat16):
    gain = level_of(key, dims, split, -0.22, 0.18) if split else 1.0
    drawn = jax.random.normal(key, dims, jnp.float32) * scale * gain
    return jnp.minimum(jnp.maximum(drawn, -bound), bound).astype(kind)


def setup_inputs(seed: int = 0) -> dict:
    key_of = jax.random.split(jax.random.key(seed), 7)
    return {
        "deltas": normal_values(key_of[0], (TOKENS, UF), 1.0, 6.0, ((0, 16), (1, 32))),
        "gradients": normal_values(key_of[1], (TOKENS, VF), TOKENS ** -0.5, 0.375, ((0, 32), (1, 16))),
        "up_blocks": draw_up_blocks(jax.random.fold_in(key_of[6], 71), 0),
        "down_blocks": draw_down_blocks(jax.random.fold_in(key_of[6], 71), 0),
        "decoder": normal_values(key_of[4], (UF, D), D ** -0.5, 0.09375, ((0, 32), (1, 16))),
        "encoder": normal_values(key_of[5], (D, VF), 1.0, 6.0, ((0, 32), (1, 16))),
    }


def reference(deltas, gradients, up_blocks, down_blocks, decoder, encoder):
    owners = (jnp.arange(N_UP * UACT, dtype=jnp.int32) // UACT) * UB_DEV
    global_ids = up_blocks + owners[None, :]
    every_block = jnp.arange(N_UP * UB_DEV, dtype=jnp.int32)
    block_on = jnp.any(global_ids[:, :, None] == every_block[None, None, :], axis=1)
    masked = deltas.reshape(WINDOWS, WIN, N_UP * UB_DEV, BLOCK) * block_on[:, None, :, None].astype(deltas.dtype)
    masked = masked.reshape(TOKENS, UF)

    def shard_scores(shard_index):
        enc_cols = lax.dynamic_slice_in_dim(encoder, shard_index * VF_DEV, VF_DEV, 1).reshape(D, VB_DEV, BLOCK)
        grad_cols = lax.dynamic_slice_in_dim(gradients, shard_index * VF_DEV, VF_DEV, 1).reshape(TOKENS, VB_DEV, BLOCK)
        chosen = lax.dynamic_slice_in_dim(down_blocks, shard_index * DACT, DACT, 0)
        enc_used = jnp.take(enc_cols, chosen, axis=1).reshape(D, DACT * BLOCK)
        grad_used = jnp.take(grad_cols, chosen, axis=1).reshape(TOKENS, DACT * BLOCK)
        virtual = jnp.dot(decoder, enc_used, preferred_element_type=jnp.float32)
        product = lax.dot_general(masked, grad_used, (((0,), (0,)), ((), ())), preferred_element_type=jnp.float32)
        scored = (product * virtual).reshape(UF, DACT, BLOCK)
        filled = jnp.zeros((UF, VB_DEV, BLOCK), jnp.float32).at[:, chosen, :].set(scored)
        return filled.reshape(UF, VF_DEV)

    stacked = lax.map(shard_scores, jnp.arange(N_DOWN, dtype=jnp.int32))
    return jnp.transpose(stacked, (1, 0, 2)).reshape(UF, VF)
```

```python
import jax
import jax.numpy as jnp
from jax import lax
from jax.experimental import pallas as pl
from jax.experimental.pallas import tpu as pltpu
from jax.sharding import Mesh
from jax.sharding import PartitionSpec as P

UF_DEV = 512
VF_DEV = 1024
BLOCK = 128
DACT = 4
UACT = 2
KD = 288
KE = 144
TD = 16
TE = 8
RD = KD + TD
RE = KE + TE
DOWN = ("xl", "y")
UP = ("z", "xh", "c")
NY = 8
VMEM = pl.BlockSpec(memory_space=pltpu.VMEM)
SMEM = pl.BlockSpec(memory_space=pltpu.SMEM)
ANY = pl.BlockSpec(memory_space=pl.ANY)


def pack_kernel(down_ref, dec_ref, delta_ref, enc_ref, grad_ref, d_ref, e_ref, active, sems):
    def move(source, target):
        copy = pltpu.make_async_copy(source, target, sems.at[len(copies)])
        copies.append(copy)
        copy.start()

    copies = []
    for i in range(DACT):
        cols = pl.ds(pl.multiple_of(down_ref[i] * BLOCK, BLOCK), BLOCK)
        move(enc_ref.at[:, cols], active.at[:KE, i * BLOCK : (i + 1) * BLOCK])
        move(grad_ref.at[:, cols], active.at[KE:, i * BLOCK : (i + 1) * BLOCK])
    first = len(copies)
    move(dec_ref, d_ref.at[:KD])
    move(delta_ref, d_ref.at[KD:])
    for copy in copies[:first]:
        copy.wait()
    for n in range(e_ref.shape[0]):
        move(active, e_ref.at[n])
    for copy in copies[first:]:
        copy.wait()


def pack(down_blocks, dec_t, deltas, encoder, gradients, copies):
    cols = DACT * BLOCK
    return pl.pallas_call(
        pack_kernel,
        out_shape=(
            jax.ShapeDtypeStruct((RD, UF_DEV), jnp.bfloat16),
            jax.ShapeDtypeStruct((copies, RE, cols), jnp.bfloat16),
        ),
        in_specs=[SMEM, ANY, ANY, ANY, ANY],
        out_specs=(VMEM, ANY),
        scratch_shapes=[
            pltpu.VMEM((RE, cols), jnp.bfloat16),
            pltpu.SemaphoreType.DMA((2 * DACT + 2 + copies,)),
        ],
        compiler_params=pltpu.CompilerParams(vmem_limit_bytes=60 << 20),
    )(down_blocks, dec_t, deltas, encoder, gradients)


def score_kernel(pos_ref, up_ref, down_ref, *refs):
    shards = refs[: NY + 1]
    own, swapped, out_ref, dec, tok, enc, grad, sems = refs[NY + 1 :]
    y, core = pos_ref[0], pos_ref[1]
    copies = []

    def fetch(source, target):
        copies.append(pltpu.make_async_copy(source, target, sems.at[len(copies)]))
        copies[-1].start()

    for source, part in ((own, core), (swapped, 1 - core)):
        fetch(source.at[:, :KE], enc.at[:, part])
        fetch(source.at[:, KE:], grad.at[:, part])
    for shard, by in zip(shards, (0, -1, 1, -2, 2, -3, 3)):
        at = lax.rem(y + by + NY, NY)
        fetch(shard.at[:, :KD], dec.at[:, at])
        fetch(shard.at[:, KD:], tok.at[:, at])
    far = lax.rem(y + NY // 2, NY)
    for xl in range(2):
        fetch(shards[NY - 1 + xl].at[0, :KD], dec.at[xl, far])
        fetch(shards[NY - 1 + xl].at[0, KD:], tok.at[xl, far])
    out_ref[...] = jnp.zeros_like(out_ref)
    for copy in copies:
        copy.wait()
    lane_block = lax.broadcasted_iota(jnp.int32, (2 * TD, UF_DEV), 1) // BLOCK
    masked = []
    for w in range(NY):
        on = (lane_block == up_ref[w, 0]) | (lane_block == up_ref[w, 1])
        delta = tok[w // 4, 2 * (w % 4) : 2 * (w % 4) + 2].reshape(2 * TD, UF_DEV)
        masked.append(jnp.where(on, delta.astype(jnp.float32), 0.0))
    masked = jnp.concatenate(masked, 0).astype(jnp.bfloat16)
    kept = grad[...].astype(jnp.float32).reshape(NY * 2 * TD, DACT * BLOCK).astype(jnp.bfloat16)
    dims = (((0,), (0,)), ((), ()))
    product = lax.dot_general(masked, kept, dims, preferred_element_type=jnp.float32)
    virtual = None
    for xl in range(2):
        term = lax.dot_general(
            dec[xl].reshape(NY * KD, UF_DEV),
            enc[xl * NY : (xl + 1) * NY].reshape(NY * KD, DACT * BLOCK),
            dims,
            preferred_element_type=jnp.float32,
        )
        virtual = term if virtual is None else virtual + term
    scored = product * virtual
    for i in range(DACT):
        cols = pl.ds(pl.multiple_of(down_ref[i] * BLOCK, BLOCK), BLOCK)
        out_ref[:, cols] = scored[:, i * BLOCK : (i + 1) * BLOCK]


def score(pos, up_blocks, down_blocks, shards, own, swapped):
    cols = DACT * BLOCK
    return pl.pallas_call(
        score_kernel,
        out_shape=jax.ShapeDtypeStruct((UF_DEV, VF_DEV), jnp.float32),
        in_specs=[SMEM, SMEM, SMEM] + [ANY] * (NY + 3),
        out_specs=VMEM,
        scratch_shapes=[
            pltpu.VMEM((2, NY, KD, UF_DEV), jnp.bfloat16),
            pltpu.VMEM((2, NY, TD, UF_DEV), jnp.bfloat16),
            pltpu.VMEM((2 * NY, 2, KE, cols), jnp.bfloat16),
            pltpu.VMEM((2 * NY, 2, TE, cols), jnp.bfloat16),
            pltpu.SemaphoreType.DMA((4 + 2 * (NY + 1),)),
        ],
        compiler_params=pltpu.CompilerParams(vmem_limit_bytes=60 << 20),
    )(pos, up_blocks, down_blocks, *shards, own, swapped)


def turn(value, axis, by):
    n = lax.axis_size(axis)
    return lax.ppermute(value, axis, [(i, (i + by) % n) for i in range(n)])


def ring(pair):
    right = left = pair
    held = [pair]
    for _ in range(NY // 2 - 1):
        right, left = turn(right, "y", 1), turn(left, "y", -1)
        held += [right, left]
    return held + [turn(right[:1], "y", 1), turn(left[1:], "y", -1)]


def local(deltas, gradients, up_blocks, down_blocks, decoder, encoder):
    d, e = pack(down_blocks, decoder.T, deltas, encoder, gradients, 16)
    own = lax.all_to_all(e, ("z", "xh"), 0, 0, tiled=True)
    pair = lax.all_gather(d, "xl", axis=0)
    shards = ring(pair)
    own, shards[5], shards[6] = lax.optimization_barrier((own, shards[5], shards[6]))
    swapped = turn(own, "c", 1)
    pos = jnp.stack([lax.axis_index("y"), lax.axis_index("c")]).astype(jnp.int32)
    return score(pos, up_blocks, down_blocks, shards, own, swapped)


def solution(mesh):
    torus = Mesh(mesh.devices.reshape(8, 2, 2, 2, 8), ("z", "xh", "c", "xl", "y"))
    return jax.shard_map(
        local,
        mesh=torus,
        in_specs=(P(DOWN, UP), P(UP, DOWN), P(None, UP), P(DOWN), P(UP, DOWN), P(UP, DOWN)),
        out_specs=P(UP, DOWN),
        check_vma=False,
    )
```

```python
import jax
import jax.numpy as jnp
from jax import lax
from jax.experimental import pallas as pl
from jax.experimental.pallas import tpu as pltpu
from jax.sharding import Mesh
from jax.sharding import PartitionSpec as P

UF_DEV = 512
VF_DEV = 1024
BLOCK = 128
DACT = 4
UACT = 2
KD = 288
KE = 144
TD = 16
TE = 8
RD = KD + TD
RE = KE + TE
DOWN = ("xl", "y")
UP = ("z", "xh", "c")
NY = 8
TURNS = (0, -1, 1, -2, 2, -3, 3, 4)
STEP = 4
VMEM = pl.BlockSpec(memory_space=pltpu.VMEM)
SMEM = pl.BlockSpec(memory_space=pltpu.SMEM)
ANY = pl.BlockSpec(memory_space=pl.ANY)


def pack_kernel(down_ref, dec_ref, delta_ref, enc_ref, grad_ref, d_ref, e_ref, sems):
    copies = []

    def move(source, target):
        copies.append(pltpu.make_async_copy(source, target, sems.at[len(copies)]))
        copies[-1].start()

    for i in range(DACT):
        cols = pl.ds(pl.multiple_of(down_ref[i] * BLOCK, BLOCK), BLOCK)
        move(enc_ref.at[:, cols], e_ref.at[:KE, i * BLOCK : (i + 1) * BLOCK])
        move(grad_ref.at[:, cols], e_ref.at[KE:, i * BLOCK : (i + 1) * BLOCK])
    move(dec_ref, d_ref.at[:KD])
    move(delta_ref, d_ref.at[KD:])
    for copy in copies:
        copy.wait()


def pack(down_blocks, dec_t, deltas, encoder, gradients):
    return pl.pallas_call(
        pack_kernel,
        out_shape=(
            jax.ShapeDtypeStruct((RD, UF_DEV), jnp.bfloat16),
            jax.ShapeDtypeStruct((RE, DACT * BLOCK), jnp.bfloat16),
        ),
        in_specs=[SMEM, ANY, ANY, ANY, ANY],
        out_specs=(VMEM, VMEM),
        scratch_shapes=[pltpu.SemaphoreType.DMA((2 * DACT + 2,))],
        compiler_params=pltpu.CompilerParams(vmem_limit_bytes=60 << 20),
    )(down_blocks, dec_t, deltas, encoder, gradients)


def score_kernel(up_ref, down_ref, *refs):
    shards = refs[: 2 * NY]
    own, swapped, out_ref, dec, tok, enc, grad, dec_sem, tok_sem, enc_sem, grad_sem = refs[2 * NY :]
    y, xl, core = lax.axis_index("y"), lax.axis_index("xl"), lax.axis_index("c")
    grads = []
    for source, part in ((own, core), (swapped, 1 - core)):
        grads.append(
            pltpu.make_async_copy(
                source.at[:, KE:], grad.at[:, part], grad_sem.at[len(grads)]
            )
        )
        grads[-1].start()
    blocks, tokens = [], []
    for slot in range(2 * NY):
        turned, column = TURNS[slot // 2], xl if slot % 2 == 0 else 1 - xl
        k = column * NY + lax.rem(y + turned + NY, NY)
        mine = [
            pltpu.make_async_copy(
                source.at[k, :KE], enc.at[slot, part], enc_sem.at[slot, i]
            )
            for i, (source, part) in enumerate(((own, core), (swapped, 1 - core)))
        ]
        mine.append(
            pltpu.make_async_copy(shards[slot].at[:KD], dec.at[slot], dec_sem.at[slot])
        )
        tokens.append(
            pltpu.make_async_copy(shards[slot].at[KD:], tok.at[k], tok_sem.at[slot])
        )
        for copy in mine + tokens[-1:]:
            copy.start()
        blocks.append(mine)
    out_ref[...] = jnp.zeros_like(out_ref)
    dims = (((0,), (0,)), ((), ()))
    virtual = None
    for first in range(0, 2 * NY, STEP):
        for slot in range(first, first + STEP):
            for copy in blocks[slot]:
                copy.wait()
        term = lax.dot_general(
            dec[first : first + STEP].reshape(STEP * KD, UF_DEV),
            enc[first : first + STEP].reshape(STEP * KD, DACT * BLOCK),
            dims,
            preferred_element_type=jnp.float32,
        )
        virtual = term if virtual is None else virtual + term
    for copy in grads + tokens:
        copy.wait()
    lane_block = lax.broadcasted_iota(jnp.int32, (2 * TD, UF_DEV), 1) // BLOCK
    masked = []
    for w in range(NY):
        on = (lane_block == up_ref[0, w]) | (lane_block == up_ref[1, w])
        delta = tok[2 * w : 2 * w + 2].reshape(2 * TD, UF_DEV)
        masked.append(jnp.where(on, delta.astype(jnp.float32), 0.0))
    masked = jnp.concatenate(masked, 0).astype(jnp.bfloat16)
    kept = grad[...].astype(jnp.float32).reshape(NY * 2 * TD, DACT * BLOCK).astype(jnp.bfloat16)
    product = lax.dot_general(masked, kept, dims, preferred_element_type=jnp.float32)
    scored = product * virtual
    for i in range(DACT):
        cols = pl.ds(pl.multiple_of(down_ref[i] * BLOCK, BLOCK), BLOCK)
        out_ref[:, cols] = scored[:, i * BLOCK : (i + 1) * BLOCK]


def score(up_blocks, down_blocks, shards, own, swapped):
    cols = DACT * BLOCK
    return pl.pallas_call(
        score_kernel,
        out_shape=jax.ShapeDtypeStruct((UF_DEV, VF_DEV), jnp.float32),
        in_specs=[SMEM, SMEM] + [ANY] * (2 * NY + 2),
        out_specs=VMEM,
        scratch_shapes=[
            pltpu.VMEM((2 * NY, KD, UF_DEV), jnp.bfloat16),
            pltpu.VMEM((2 * NY, TD, UF_DEV), jnp.bfloat16),
            pltpu.VMEM((2 * NY, 2, KE, cols), jnp.bfloat16),
            pltpu.VMEM((2 * NY, 2, TE, cols), jnp.bfloat16),
            pltpu.SemaphoreType.DMA((2 * NY,)),
            pltpu.SemaphoreType.DMA((2 * NY,)),
            pltpu.SemaphoreType.DMA((2 * NY, 2)),
            pltpu.SemaphoreType.DMA((2,)),
        ],
        compiler_params=pltpu.CompilerParams(vmem_limit_bytes=60 << 20),
    )(up_blocks.T, down_blocks, *shards, own, swapped)


def turn(value, axis, by):
    n = lax.axis_size(axis)
    return lax.ppermute(value, axis, [(i, (i + by) % n) for i in range(n)])


def ring(value, last):
    right = left = value
    held = [value]
    for _ in range(NY // 2 - 1):
        right, left = turn(right, "y", 1), turn(left, "y", -1)
        held += [right, left]
    return held + [turn(right if last > 0 else left, "y", last)]


def local(deltas, gradients, up_blocks, down_blocks, decoder, encoder):
    d, e = pack(down_blocks, decoder.T, deltas, encoder, gradients)
    pair = lax.all_gather(e, "xh")
    own = lax.all_to_all(jnp.broadcast_to(pair[None], (NY, *pair.shape)), "z", 0, 0, tiled=True)
    near = ring(d, 1)
    across = ring(turn(d, "xl", 1), -1)
    own, near[5:], across[5:7] = lax.optimization_barrier((own, near[5:], across[5:7]))
    shards = [shard for both in zip(near, across) for shard in both]
    swapped = turn(own, "c", 1)
    own, swapped = (v.reshape(2 * NY, RE, DACT * BLOCK) for v in (own, swapped))
    return score(up_blocks, down_blocks, shards, own, swapped)


def solution(mesh):
    torus = Mesh(mesh.devices.reshape(8, 2, 2, 2, 8), ("z", "xh", "c", "xl", "y"))
    return jax.shard_map(
        local,
        mesh=torus,
        in_specs=(P(DOWN, UP), P(UP, DOWN), P(None, UP), P(DOWN), P(UP, DOWN), P(UP, DOWN)),
        out_specs=P(UP, DOWN),
        check_vma=False,
    )
```

```python
import jax
import jax.numpy as jnp
from jax import lax
from jax.experimental import pallas as pl
from jax.experimental.pallas import tpu as pltpu
from jax.sharding import Mesh
from jax.sharding import PartitionSpec as P

UF_DEV = 512
VF_DEV = 1024
BLOCK = 128
DACT = 4
UACT = 2
KD = 288
KE = 144
TD = 16
TE = 8
RD = KD + TD
RE = KE + TE
DOWN = ("xl", "y")
UP = ("z", "xh", "c")
NY = 8
TURNS = (0, -1, 1, -2, 2, -3, 3, 4)
STEP = 4
VMEM = pl.BlockSpec(memory_space=pltpu.VMEM)
SMEM = pl.BlockSpec(memory_space=pltpu.SMEM)
ANY = pl.BlockSpec(memory_space=pl.ANY)


def pack_kernel(down_ref, dec_ref, delta_ref, enc_ref, grad_ref, d_ref, e_ref, active, sems):
    copies = []

    def move(source, target):
        copies.append(pltpu.make_async_copy(source, target, sems.at[len(copies)]))
        copies[-1].start()

    for i in range(DACT):
        cols = pl.ds(pl.multiple_of(down_ref[i] * BLOCK, BLOCK), BLOCK)
        move(enc_ref.at[:, cols], active.at[:KE, i * BLOCK : (i + 1) * BLOCK])
        move(grad_ref.at[:, cols], active.at[KE:, i * BLOCK : (i + 1) * BLOCK])
    loads = len(copies)
    move(dec_ref, d_ref.at[:KD])
    move(delta_ref, d_ref.at[KD:])
    for copy in copies[:loads]:
        copy.wait()
    for n in range(2 * NY):
        move(active, e_ref.at[n])
    for copy in copies[loads:]:
        copy.wait()


def pack(down_blocks, dec_t, deltas, encoder, gradients):
    return pl.pallas_call(
        pack_kernel,
        out_shape=(
            jax.ShapeDtypeStruct((RD, UF_DEV), jnp.bfloat16),
            jax.ShapeDtypeStruct((2 * NY, RE, DACT * BLOCK), jnp.bfloat16),
        ),
        in_specs=[SMEM, ANY, ANY, ANY, ANY],
        out_specs=(VMEM, ANY),
        scratch_shapes=[
            pltpu.VMEM((RE, DACT * BLOCK), jnp.bfloat16),
            pltpu.SemaphoreType.DMA((2 * DACT + 2 + 2 * NY,)),
        ],
        compiler_params=pltpu.CompilerParams(vmem_limit_bytes=60 << 20),
    )(down_blocks, dec_t, deltas, encoder, gradients)


def score_kernel(up_ref, down_ref, *refs):
    shards = refs[: 2 * NY]
    own, swapped, out_ref, dec, tok, enc, grad, zero, scored = refs[2 * NY : 2 * NY + 9]
    dec_sem, tok_sem, enc_sem, grad_sem, zero_sem, out_sem = refs[2 * NY + 9 :]
    y, xl, core = lax.axis_index("y"), lax.axis_index("xl"), lax.axis_index("c")
    grads = []
    for source, part in ((own, core), (swapped, 1 - core)):
        grads.append(
            pltpu.make_async_copy(
                source.at[:, KE:], grad.at[:, part], grad_sem.at[len(grads)]
            )
        )
        grads[-1].start()
    blocks, tokens = [], []
    for slot in range(2 * NY):
        turned, column = TURNS[slot // 2], xl if slot % 2 == 0 else 1 - xl
        k = column * NY + lax.rem(y + turned + NY, NY)
        mine = [
            pltpu.make_async_copy(
                source.at[k, :KE], enc.at[slot, part], enc_sem.at[slot, i]
            )
            for i, (source, part) in enumerate(((own, core), (swapped, 1 - core)))
        ]
        mine.append(
            pltpu.make_async_copy(shards[slot].at[:KD], dec.at[slot], dec_sem.at[slot])
        )
        tokens.append(
            pltpu.make_async_copy(shards[slot].at[KD:], tok.at[k], tok_sem.at[slot])
        )
        for copy in mine + tokens[-1:]:
            copy.start()
        blocks.append(mine)
    zero[...] = jnp.zeros_like(zero)

    def blank(b):
        return pltpu.make_async_copy(
            zero, out_ref.at[:, b * BLOCK : (b + 1) * BLOCK], zero_sem.at[b]
        )

    idle = []
    for b in range(VF_DEV // BLOCK):
        used = down_ref[0] == b
        for i in range(1, DACT):
            used = used | (down_ref[i] == b)
        idle.append(jnp.logical_not(used))
        pl.when(idle[b])(blank(b).start)
    dims = (((0,), (0,)), ((), ()))
    virtual = None
    for first in range(0, 2 * NY, STEP):
        for slot in range(first, first + STEP):
            for copy in blocks[slot]:
                copy.wait()
        term = lax.dot_general(
            dec[first : first + STEP].reshape(STEP * KD, UF_DEV),
            enc[first : first + STEP].reshape(STEP * KD, DACT * BLOCK),
            dims,
            preferred_element_type=jnp.float32,
        )
        virtual = term if virtual is None else virtual + term
    for copy in grads + tokens:
        copy.wait()
    lane_block = lax.broadcasted_iota(jnp.int32, (2 * TD, UF_DEV), 1) // BLOCK
    masked = []
    for w in range(NY):
        on = (lane_block == up_ref[0, w]) | (lane_block == up_ref[1, w])
        delta = tok[2 * w : 2 * w + 2].reshape(2 * TD, UF_DEV)
        masked.append(jnp.where(on, delta.astype(jnp.float32), 0.0))
    masked = jnp.concatenate(masked, 0).astype(jnp.bfloat16)
    kept = grad[...].astype(jnp.float32).reshape(NY * 2 * TD, DACT * BLOCK).astype(jnp.bfloat16)
    product = lax.dot_general(masked, kept, dims, preferred_element_type=jnp.float32)
    filled = []
    for i in range(DACT):
        part = slice(i * BLOCK, (i + 1) * BLOCK)
        scored[i] = product[:, part] * virtual[:, part]
        cols = pl.ds(pl.multiple_of(down_ref[i] * BLOCK, BLOCK), BLOCK)
        filled.append(
            pltpu.make_async_copy(scored.at[i], out_ref.at[:, cols], out_sem.at[i])
        )
        filled[i].start()
    for b in range(VF_DEV // BLOCK):
        pl.when(idle[b])(blank(b).wait)
    for copy in filled:
        copy.wait()


def score(up_blocks, down_blocks, shards, own, swapped):
    cols = DACT * BLOCK
    return pl.pallas_call(
        score_kernel,
        out_shape=jax.ShapeDtypeStruct((UF_DEV, VF_DEV), jnp.float32),
        in_specs=[SMEM, SMEM] + [ANY] * (2 * NY + 2),
        out_specs=ANY,
        scratch_shapes=[
            pltpu.VMEM((2 * NY, KD, UF_DEV), jnp.bfloat16),
            pltpu.VMEM((2 * NY, TD, UF_DEV), jnp.bfloat16),
            pltpu.VMEM((2 * NY, 2, KE, cols), jnp.bfloat16),
            pltpu.VMEM((2 * NY, 2, TE, cols), jnp.bfloat16),
            pltpu.VMEM((UF_DEV, BLOCK), jnp.float32),
            pltpu.VMEM((DACT, UF_DEV, BLOCK), jnp.float32),
            pltpu.SemaphoreType.DMA((2 * NY,)),
            pltpu.SemaphoreType.DMA((2 * NY,)),
            pltpu.SemaphoreType.DMA((2 * NY, 2)),
            pltpu.SemaphoreType.DMA((2,)),
            pltpu.SemaphoreType.DMA((VF_DEV // BLOCK,)),
            pltpu.SemaphoreType.DMA((DACT,)),
        ],
        compiler_params=pltpu.CompilerParams(vmem_limit_bytes=60 << 20),
    )(up_blocks.T, down_blocks, *shards, own, swapped)


def turn(value, axis, by):
    n = lax.axis_size(axis)
    return lax.ppermute(value, axis, [(i, (i + by) % n) for i in range(n)])


def ring(value):
    right = left = value
    held = [value]
    for _ in range(NY // 2 - 1):
        right, left = turn(right, "y", 1), turn(left, "y", -1)
        held += [right, left]
    return held


def local(deltas, gradients, up_blocks, down_blocks, decoder, encoder):
    d, e = pack(down_blocks, decoder.T, deltas, encoder, gradients)
    own = lax.all_to_all(e, ("z", "xh"), 0, 0, tiled=True)
    near = ring(d)
    across = ring(turn(d, "xl", 1))
    far = turn(near[5], "y", 1)
    beyond = turn(far, "xl", 1)
    own, last, near[5:], across[5:] = lax.optimization_barrier((own, far, near[5:], across[5:]))
    shards = [s for both in zip(near + [last], across + [beyond]) for s in both]
    swapped = turn(own, "c", 1)
    return score(up_blocks, down_blocks, shards, own, swapped)


def solution(mesh):
    torus = Mesh(mesh.devices.reshape(8, 2, 2, 2, 8), ("z", "xh", "c", "xl", "y"))
    return jax.shard_map(
        local,
        mesh=torus,
        in_specs=(P(DOWN, UP), P(UP, DOWN), P(None, UP), P(DOWN), P(UP, DOWN), P(UP, DOWN)),
        out_specs=P(UP, DOWN),
        check_vma=False,
    )
```

```python
import jax
import jax.numpy as jnp
from jax import lax
from jax.experimental import pallas as pl
from jax.experimental.pallas import tpu as pltpu
from jax.sharding import Mesh
from jax.sharding import PartitionSpec as P

UF_DEV = 512
VF_DEV = 1024
BLOCK = 128
DACT = 4
UACT = 2
KD = 288
KE = 144
TD = 16
TE = 8
RD = KD + TD
RE = KE + TE
DOWN = ("xl", "y")
UP = ("z", "xh", "c")
NY = 8
TURNS = (0, -1, 1, -2, 2, -3, 3, 4)
STEP = 4
VMEM = pl.BlockSpec(memory_space=pltpu.VMEM)
SMEM = pl.BlockSpec(memory_space=pltpu.SMEM)
ANY = pl.BlockSpec(memory_space=pl.ANY)


def pack_kernel(down_ref, dec_ref, delta_ref, enc_ref, grad_ref, d_ref, e_ref, active, sems):
    copies = []

    def move(source, target):
        copies.append(pltpu.make_async_copy(source, target, sems.at[len(copies)]))
        copies[-1].start()

    for i in range(DACT):
        cols = pl.ds(pl.multiple_of(down_ref[i] * BLOCK, BLOCK), BLOCK)
        move(enc_ref.at[:, cols], active.at[:KE, i * BLOCK : (i + 1) * BLOCK])
        move(grad_ref.at[:, cols], active.at[KE:, i * BLOCK : (i + 1) * BLOCK])
    loads = len(copies)
    move(dec_ref, d_ref.at[:KD])
    move(delta_ref, d_ref.at[KD:])
    for copy in copies[:loads]:
        copy.wait()
    for n in range(2 * NY):
        move(active, e_ref.at[n])
    for copy in copies[loads:]:
        copy.wait()


def pack(down_blocks, dec_t, deltas, encoder, gradients):
    return pl.pallas_call(
        pack_kernel,
        out_shape=(
            jax.ShapeDtypeStruct((RD, UF_DEV), jnp.bfloat16),
            jax.ShapeDtypeStruct((2 * NY, RE, DACT * BLOCK), jnp.bfloat16),
        ),
        in_specs=[SMEM, ANY, ANY, ANY, ANY],
        out_specs=(VMEM, ANY),
        scratch_shapes=[
            pltpu.VMEM((RE, DACT * BLOCK), jnp.bfloat16),
            pltpu.SemaphoreType.DMA((2 * DACT + 2 + 2 * NY,)),
        ],
        compiler_params=pltpu.CompilerParams(vmem_limit_bytes=60 << 20),
    )(down_blocks, dec_t, deltas, encoder, gradients)


def accumulate(part, up_ref, shards, source, held, sems):
    dec, tok, enc, grad = held
    dec_sem, tok_sem, enc_sem, grad_sem = sems
    y, xl = lax.axis_index("y"), lax.axis_index("xl")
    rows = pl.ds(pl.multiple_of(part * KE, 16), KE)
    tokens = pl.ds(pl.multiple_of(KD + part * TE, TE), TE)
    rest = [pltpu.make_async_copy(source.at[:, KE:], grad, grad_sem)]
    blocks = []
    for slot, shard in enumerate(shards):
        column = xl if slot % 2 == 0 else 1 - xl
        k = column * NY + lax.rem(y + TURNS[slot // 2] + NY, NY)
        blocks.append(
            (
                pltpu.make_async_copy(shard.at[rows], dec.at[slot], dec_sem.at[slot]),
                pltpu.make_async_copy(source.at[k, :KE], enc.at[slot], enc_sem.at[slot]),
            )
        )
        rest.append(pltpu.make_async_copy(shard.at[tokens], tok.at[k], tok_sem.at[slot]))
        for copy in blocks[slot]:
            copy.start()
    for copy in rest:
        copy.start()
    dims = (((0,), (0,)), ((), ()))
    cols = DACT * BLOCK
    virtual = None
    for low in range(0, 2 * NY, STEP):
        for slot in range(low, low + STEP):
            for copy in blocks[slot]:
                copy.wait()
        term = lax.dot_general(
            dec[low : low + STEP].reshape(STEP * KE, UF_DEV),
            enc[low : low + STEP].reshape(STEP * KE, cols),
            dims,
            preferred_element_type=jnp.float32,
        )
        virtual = term if virtual is None else virtual + term
    for copy in rest:
        copy.wait()
    lane_block = lax.broadcasted_iota(jnp.int32, (2 * TE, UF_DEV), 1) // BLOCK
    masked = []
    for w in range(NY):
        on = (lane_block == up_ref[0, w]) | (lane_block == up_ref[1, w])
        delta = tok[2 * w : 2 * w + 2].astype(jnp.float32).reshape(2 * TE, UF_DEV)
        masked.append(jnp.where(on, delta, 0.0))
    masked = jnp.concatenate(masked, 0).astype(jnp.bfloat16)
    kept = grad[...].astype(jnp.float32).reshape(2 * NY * TE, cols).astype(jnp.bfloat16)
    product = lax.dot_general(masked, kept, dims, preferred_element_type=jnp.float32)
    return virtual, product


def half_kernel(up_ref, *refs):
    shards, (source, virtual_ref, product_ref) = refs[: 2 * NY], refs[2 * NY : 2 * NY + 3]
    held, sems = refs[2 * NY + 3 : 2 * NY + 7], refs[2 * NY + 7 :]
    virtual_ref[...], product_ref[...] = accumulate(
        lax.axis_index("c"), up_ref, shards, source, held, sems
    )


def score_kernel(up_ref, down_ref, *refs):
    shards, refs = refs[: 2 * NY], refs[2 * NY :]
    source, virtual_in, product_in, out_ref = refs[:4]
    held, sems = refs[4:8], refs[8:12]
    virtual, product, zero, scored, in_sem, zero_sem, out_sem = refs[12:]
    zero[...] = jnp.zeros_like(zero)

    def blank(b):
        return pltpu.make_async_copy(
            zero, out_ref.at[:, b * BLOCK : (b + 1) * BLOCK], zero_sem.at[b]
        )

    idle = []
    for b in range(VF_DEV // BLOCK):
        used = down_ref[0] == b
        for i in range(1, DACT):
            used = used | (down_ref[i] == b)
        idle.append(jnp.logical_not(used))
    loads = [
        pltpu.make_async_copy(virtual_in, virtual, in_sem.at[0]),
        pltpu.make_async_copy(product_in, product, in_sem.at[1]),
    ]
    for copy in loads:
        copy.start()
    more, part = accumulate(1 - lax.axis_index("c"), up_ref, shards, source, held, sems)
    for b in range(VF_DEV // BLOCK):
        pl.when(idle[b])(blank(b).start)
    for copy in loads:
        copy.wait()
    filled = []
    for i in range(DACT):
        at = slice(i * BLOCK, (i + 1) * BLOCK)
        scored[i] = (product[:, at] + part[:, at]) * (virtual[:, at] + more[:, at])
        where = pl.ds(pl.multiple_of(down_ref[i] * BLOCK, BLOCK), BLOCK)
        filled.append(
            pltpu.make_async_copy(scored.at[i], out_ref.at[:, where], out_sem.at[i])
        )
        filled[i].start()
    for b in range(VF_DEV // BLOCK):
        pl.when(idle[b])(blank(b).wait)
    for copy in filled:
        copy.wait()


COLS = DACT * BLOCK
HELD = [
    pltpu.VMEM((2 * NY, KE, UF_DEV), jnp.bfloat16),
    pltpu.VMEM((2 * NY, TE, UF_DEV), jnp.bfloat16),
    pltpu.VMEM((2 * NY, KE, COLS), jnp.bfloat16),
    pltpu.VMEM((2 * NY, TE, COLS), jnp.bfloat16),
    pltpu.SemaphoreType.DMA((2 * NY,)),
    pltpu.SemaphoreType.DMA((2 * NY,)),
    pltpu.SemaphoreType.DMA((2 * NY,)),
    pltpu.SemaphoreType.DMA,
]
COST = pl.CostEstimate(
    flops=UF_DEV * COLS * KD * 2 * NY, bytes_accessed=8 << 20, transcendentals=0
)


def half(up_t, shards, source):
    return pl.pallas_call(
        half_kernel,
        out_shape=(jax.ShapeDtypeStruct((UF_DEV, COLS), jnp.float32),) * 2,
        in_specs=[SMEM] + [ANY] * (2 * NY + 1),
        out_specs=(VMEM, VMEM),
        scratch_shapes=HELD,
        compiler_params=pltpu.CompilerParams(vmem_limit_bytes=60 << 20),
        cost_estimate=COST,
    )(up_t, *shards, source)


def score(up_t, down_blocks, shards, source, sums):
    return pl.pallas_call(
        score_kernel,
        out_shape=jax.ShapeDtypeStruct((UF_DEV, VF_DEV), jnp.float32),
        in_specs=[SMEM, SMEM] + [ANY] * (2 * NY + 3),
        out_specs=ANY,
        scratch_shapes=[
            *HELD,
            pltpu.VMEM((UF_DEV, COLS), jnp.float32),
            pltpu.VMEM((UF_DEV, COLS), jnp.float32),
            pltpu.VMEM((UF_DEV, BLOCK), jnp.float32),
            pltpu.VMEM((DACT, UF_DEV, BLOCK), jnp.float32),
            pltpu.SemaphoreType.DMA((2,)),
            pltpu.SemaphoreType.DMA((VF_DEV // BLOCK,)),
            pltpu.SemaphoreType.DMA((DACT,)),
        ],
        compiler_params=pltpu.CompilerParams(vmem_limit_bytes=60 << 20),
        cost_estimate=COST,
    )(up_t, down_blocks, *shards, source, *sums)


def turn(value, axis, by):
    n = lax.axis_size(axis)
    return lax.ppermute(value, axis, [(i, (i + by) % n) for i in range(n)])


def ring(value):
    right = left = value
    held = [value]
    for _ in range(NY // 2 - 1):
        right, left = turn(right, "y", 1), turn(left, "y", -1)
        held += [right, left]
    return held


def local(deltas, gradients, up_blocks, down_blocks, decoder, encoder):
    d, e = pack(down_blocks, decoder.T, deltas, encoder, gradients)
    own = lax.all_to_all(e, ("z", "xh"), 0, 0, tiled=True)
    near = ring(d)
    across = ring(turn(d, "xl", 1))
    far = turn(near[5], "y", 1)
    beyond = turn(far, "xl", 1)
    near, across = near + [far], across + [beyond]
    own, near[5:], across[5:] = lax.optimization_barrier((own, near[5:], across[5:]))
    shards = [shard for both in zip(near, across) for shard in both]
    swapped = turn(own, "c", 1)
    up_t = up_blocks.T
    return score(up_t, down_blocks, shards, swapped, half(up_t, shards, own))


def solution(mesh):
    torus = Mesh(mesh.devices.reshape(8, 2, 2, 2, 8), ("z", "xh", "c", "xl", "y"))
    return jax.shard_map(
        local,
        mesh=torus,
        in_specs=(P(DOWN, UP), P(UP, DOWN), P(None, UP), P(DOWN), P(UP, DOWN), P(UP, DOWN)),
        out_specs=P(UP, DOWN),
        check_vma=False,
    )
```

```python
import jax
import jax.numpy as jnp
from jax import lax
from jax.experimental import pallas as pl
from jax.experimental.pallas import tpu as pltpu
from jax.sharding import Mesh
from jax.sharding import PartitionSpec as P

UF_DEV = 512
VF_DEV = 1024
BLOCK = 128
DACT = 4
UACT = 2
KD = 288
KE = 144
TD = 16
TE = 8
RD = KD + TD
RE = KE + TE
DOWN = ("xl", "y")
UP = ("z", "xh", "c")
NY = 8
TURNS = (0, -1, 1, -2, 2, -3, 3, 4)
STEP = 4
VMEM = pl.BlockSpec(memory_space=pltpu.VMEM)
SMEM = pl.BlockSpec(memory_space=pltpu.SMEM)
ANY = pl.BlockSpec(memory_space=pl.ANY)


def pack_kernel(down_ref, dec_ref, delta_ref, enc_ref, grad_ref, d_ref, e_ref, active, sems):
    copies = []

    def move(source, target):
        copies.append(pltpu.make_async_copy(source, target, sems.at[len(copies)]))
        copies[-1].start()

    for i in range(DACT):
        cols = pl.ds(pl.multiple_of(down_ref[i] * BLOCK, BLOCK), BLOCK)
        move(enc_ref.at[:, cols], active.at[:KE, i * BLOCK : (i + 1) * BLOCK])
        move(grad_ref.at[:, cols], active.at[KE:, i * BLOCK : (i + 1) * BLOCK])
    loads = len(copies)
    move(dec_ref, d_ref.at[:KD])
    move(delta_ref, d_ref.at[KD:])
    for copy in copies[:loads]:
        copy.wait()
    for n in range(2 * NY):
        move(active, e_ref.at[n])
    for copy in copies[loads:]:
        copy.wait()


def pack(down_blocks, dec_t, deltas, encoder, gradients):
    return pl.pallas_call(
        pack_kernel,
        out_shape=(
            jax.ShapeDtypeStruct((RD, UF_DEV), jnp.bfloat16),
            jax.ShapeDtypeStruct((2 * NY, RE, DACT * BLOCK), jnp.bfloat16),
        ),
        in_specs=[SMEM, ANY, ANY, ANY, ANY],
        out_specs=(VMEM, ANY),
        scratch_shapes=[
            pltpu.VMEM((RE, DACT * BLOCK), jnp.bfloat16),
            pltpu.SemaphoreType.DMA((2 * DACT + 2 + 2 * NY,)),
        ],
        compiler_params=pltpu.CompilerParams(vmem_limit_bytes=60 << 20),
    )(down_blocks, dec_t, deltas, encoder, gradients)


def accumulate(items, up_ref, dec, enc, dec_sem, enc_sem):
    chunks = [range(low, min(low + STEP, len(items))) for low in range(0, len(items), STEP)]
    if len(chunks[-1]) == 1:
        chunks[-2:] = [range(chunks[-2].start, len(items))]
    for n, chunk in enumerate(chunks):
        for slot in chunk:
            shard, k, part, source = items[slot]
            rows = pl.ds(pl.multiple_of(part * KE, 16), KE)
            tokens = pl.ds(pl.multiple_of(KD + part * TE, TE), TE)
            here = dec.at[slot]
            pltpu.make_async_copy(source.at[k], enc.at[slot], enc_sem.at[n]).start()
            pltpu.make_async_copy(shard.at[rows], here.at[:KE], dec_sem.at[n]).start()
            pltpu.make_async_copy(shard.at[tokens], here.at[KE:], dec_sem.at[n]).start()
    dims = (((0,), (0,)), ((), ()))
    cols = DACT * BLOCK
    virtual = None
    for n, chunk in enumerate(chunks):
        at = slice(chunk.start, chunk.stop)
        pltpu.make_async_copy(dec.at[at], dec.at[at], dec_sem.at[n]).wait()
        pltpu.make_async_copy(enc.at[at], enc.at[at], enc_sem.at[n]).wait()
        term = lax.dot_general(
            dec[at, :KE].reshape(len(chunk) * KE, UF_DEV),
            enc[at, :KE].reshape(len(chunk) * KE, cols),
            dims,
            preferred_element_type=jnp.float32,
        )
        virtual = term if virtual is None else virtual + term
    lane_block = lax.broadcasted_iota(jnp.int32, (TE, UF_DEV), 1) // BLOCK
    masked, kept = [], []
    for slot, (_, k, _, _) in enumerate(items):
        w = k // 2
        on = (lane_block == up_ref[0, w]) | (lane_block == up_ref[1, w])
        masked.append(jnp.where(on, dec[slot, KE:].astype(jnp.float32), 0.0))
        kept.append(enc[slot, KE:].astype(jnp.float32))
    masked, kept = (jnp.concatenate(v, 0).astype(jnp.bfloat16) for v in (masked, kept))
    product = lax.dot_general(masked, kept, dims, preferred_element_type=jnp.float32)
    return virtual, product


def places():
    y, xl = lax.axis_index("y"), lax.axis_index("xl")
    return [
        (xl if slot % 2 == 0 else 1 - xl) * NY + lax.rem(y + TURNS[slot // 2] + NY, NY)
        for slot in range(2 * NY)
    ]


def half_kernel(up_ref, *refs):
    shards, refs = refs[: 2 * NY - 1], refs[2 * NY - 1 :]
    source, virtual_ref, product_ref, dec, enc, dec_sem, enc_sem = refs
    core = lax.axis_index("c")
    items = [(shard, k, core, source) for shard, k in zip(shards, places())]
    virtual_ref[...], product_ref[...] = accumulate(
        items, up_ref, dec, enc, dec_sem, enc_sem
    )


def score_kernel(up_ref, down_ref, *refs):
    shards, refs = refs[: 2 * NY], refs[2 * NY :]
    own, swapped, virtual_in, product_in, out_ref = refs[:5]
    dec, enc, dec_sem, enc_sem, virtual, product, zero, scored = refs[5:13]
    in_sem, zero_sem, out_sem = refs[13:]
    zero[...] = jnp.zeros_like(zero)

    def blank(b):
        return pltpu.make_async_copy(
            zero, out_ref.at[:, b * BLOCK : (b + 1) * BLOCK], zero_sem.at[b]
        )

    idle = []
    for b in range(VF_DEV // BLOCK):
        used = down_ref[0] == b
        for i in range(1, DACT):
            used = used | (down_ref[i] == b)
        idle.append(jnp.logical_not(used))
    loads = [
        pltpu.make_async_copy(virtual_in, virtual, in_sem.at[0]),
        pltpu.make_async_copy(product_in, product, in_sem.at[1]),
    ]
    for copy in loads:
        copy.start()
    core, ks = lax.axis_index("c"), places()
    items = [(shard, k, 1 - core, swapped) for shard, k in zip(shards, ks)]
    items.append((shards[-1], ks[-1], core, own))
    more, part = accumulate(items, up_ref, dec, enc, dec_sem, enc_sem)
    for b in range(VF_DEV // BLOCK):
        pl.when(idle[b])(blank(b).start)
    for copy in loads:
        copy.wait()
    filled = []
    for i in range(DACT):
        at = slice(i * BLOCK, (i + 1) * BLOCK)
        scored[i] = (product[:, at] + part[:, at]) * (virtual[:, at] + more[:, at])
        where = pl.ds(pl.multiple_of(down_ref[i] * BLOCK, BLOCK), BLOCK)
        filled.append(
            pltpu.make_async_copy(scored.at[i], out_ref.at[:, where], out_sem.at[i])
        )
        filled[i].start()
    for b in range(VF_DEV // BLOCK):
        pl.when(idle[b])(blank(b).wait)
    for copy in filled:
        copy.wait()


COLS = DACT * BLOCK


def held(count):
    return [
        pltpu.VMEM((count, RE, UF_DEV), jnp.bfloat16),
        pltpu.VMEM((count, RE, COLS), jnp.bfloat16),
        pltpu.SemaphoreType.DMA((-(-count // STEP),)),
        pltpu.SemaphoreType.DMA((-(-count // STEP),)),
    ]


COST = pl.CostEstimate(
    flops=UF_DEV * COLS * KD * 2 * NY, bytes_accessed=8 << 20, transcendentals=0
)


def half(up_t, shards, source):
    return pl.pallas_call(
        half_kernel,
        out_shape=(jax.ShapeDtypeStruct((UF_DEV, COLS), jnp.float32),) * 2,
        in_specs=[SMEM] + [ANY] * (2 * NY),
        out_specs=(VMEM, VMEM),
        scratch_shapes=held(2 * NY - 1),
        compiler_params=pltpu.CompilerParams(vmem_limit_bytes=60 << 20),
        cost_estimate=COST,
    )(up_t, *shards, source)


def score(up_t, down_blocks, shards, own, swapped, sums):
    return pl.pallas_call(
        score_kernel,
        out_shape=jax.ShapeDtypeStruct((UF_DEV, VF_DEV), jnp.float32),
        in_specs=[SMEM, SMEM] + [ANY] * (2 * NY + 4),
        out_specs=ANY,
        scratch_shapes=[
            *held(2 * NY + 1),
            pltpu.VMEM((UF_DEV, COLS), jnp.float32),
            pltpu.VMEM((UF_DEV, COLS), jnp.float32),
            pltpu.VMEM((UF_DEV, BLOCK), jnp.float32),
            pltpu.VMEM((DACT, UF_DEV, BLOCK), jnp.float32),
            pltpu.SemaphoreType.DMA((2,)),
            pltpu.SemaphoreType.DMA((VF_DEV // BLOCK,)),
            pltpu.SemaphoreType.DMA((DACT,)),
        ],
        compiler_params=pltpu.CompilerParams(vmem_limit_bytes=60 << 20),
        cost_estimate=COST,
    )(up_t, down_blocks, *shards, own, swapped, *sums)


def turn(value, axis, by):
    n = lax.axis_size(axis)
    return lax.ppermute(value, axis, [(i, (i + by) % n) for i in range(n)])


def step(right, left):
    return turn(right, "y", 1), turn(left, "y", -1)


def local(deltas, gradients, up_blocks, down_blocks, decoder, encoder):
    d, e = pack(down_blocks, decoder.T, deltas, encoder, gradients)
    own = lax.all_to_all(e, ("z", "xh"), 0, 0, tiled=True)
    a1 = step(d, d)
    b0 = turn(d, "xl", 1)
    a2 = step(*a1)
    a3 = step(*a2)
    b1 = step(b0, b0)
    b2 = step(*b1)
    b3 = step(*b2)
    a4 = turn(a3[0], "y", 1)
    b4 = turn(a4, "xl", 1)
    own, a3, a4, b3, b4 = lax.optimization_barrier((own, a3, a4, b3, b4))
    near, across = [d, *a1, *a2, *a3, a4], [b0, *b1, *b2, *b3, b4]
    shards = [shard for both in zip(near, across) for shard in both]
    swapped = turn(own, "c", 1)
    up_t = up_blocks.T
    sums = half(up_t, shards[:-1], own)
    return score(up_t, down_blocks, shards, own, swapped, sums)


def solution(mesh):
    torus = Mesh(mesh.devices.reshape(8, 2, 2, 2, 8), ("z", "xh", "c", "xl", "y"))
    return jax.shard_map(
        local,
        mesh=torus,
        in_specs=(P(DOWN, UP), P(UP, DOWN), P(None, UP), P(DOWN), P(UP, DOWN), P(UP, DOWN)),
        out_specs=P(UP, DOWN),
        check_vma=False,
    )
```

```python
import jax
import jax.numpy as jnp
from jax import lax
from jax.experimental import pallas as pl
from jax.experimental.pallas import tpu as pltpu
from jax.sharding import Mesh
from jax.sharding import PartitionSpec as P

UF_DEV = 512
VF_DEV = 1024
BLOCK = 128
DACT = 4
UACT = 2
KD = 288
KE = 144
TD = 16
TE = 8
RD = KD + TD
RE = KE + TE
DOWN = ("xl", "y")
UP = ("z", "xh", "c")
NY = 8
TURNS = (0, -1, 1, -2, 2, -3, 3, 4)
STEP = 4
DIMS = (((0,), (0,)), ((), ()))
VMEM = pl.BlockSpec(memory_space=pltpu.VMEM)
SMEM = pl.BlockSpec(memory_space=pltpu.SMEM)
ANY = pl.BlockSpec(memory_space=pl.ANY)


def pack_kernel(down_ref, dec_ref, delta_ref, enc_ref, grad_ref, d_ref, e_ref, active, sems):
    copies = []

    def move(source, target):
        copies.append(pltpu.make_async_copy(source, target, sems.at[len(copies)]))
        copies[-1].start()

    for i in range(DACT):
        cols = pl.ds(pl.multiple_of(down_ref[i] * BLOCK, BLOCK), BLOCK)
        move(enc_ref.at[:, cols], active.at[:KE, i * BLOCK : (i + 1) * BLOCK])
        move(grad_ref.at[:, cols], active.at[KE:, i * BLOCK : (i + 1) * BLOCK])
    loads = len(copies)
    move(dec_ref, d_ref.at[:KD])
    move(delta_ref, d_ref.at[KD:])
    for copy in copies[:loads]:
        copy.wait()
    for n in range(2 * NY):
        move(active, e_ref.at[n])
    for copy in copies[loads:]:
        copy.wait()


def pack(down_blocks, dec_t, deltas, encoder, gradients):
    return pl.pallas_call(
        pack_kernel,
        out_shape=(
            jax.ShapeDtypeStruct((RD, UF_DEV), jnp.bfloat16),
            jax.ShapeDtypeStruct((2 * NY, RE, DACT * BLOCK), jnp.bfloat16),
        ),
        in_specs=[SMEM, ANY, ANY, ANY, ANY],
        out_specs=(VMEM, ANY),
        scratch_shapes=[
            pltpu.VMEM((RE, DACT * BLOCK), jnp.bfloat16),
            pltpu.SemaphoreType.DMA((2 * DACT + 2 + 2 * NY,)),
        ],
        compiler_params=pltpu.CompilerParams(vmem_limit_bytes=60 << 20),
    )(down_blocks, dec_t, deltas, encoder, gradients)


def accumulate(items, tokens, dec, enc, dec_sem, enc_sem):
    chunks = [range(low, min(low + STEP, len(items))) for low in range(0, len(items), STEP)]
    if len(chunks[-1]) == 1:
        chunks[-2:] = [range(chunks[-2].start, len(items))]
    for n, chunk in enumerate(chunks):
        for slot in chunk:
            shard, k, part, source = items[slot]
            rows = pl.ds(pl.multiple_of(part * KE, 16), KE)
            here = dec.at[slot]
            pltpu.make_async_copy(
                source.at[k, : enc.shape[1]], enc.at[slot], enc_sem.at[n]
            ).start()
            pltpu.make_async_copy(shard.at[rows], here.at[:KE], dec_sem.at[n]).start()
            if tokens:
                pltpu.make_async_copy(shard.at[KD:], here.at[KE:], dec_sem.at[n]).start()
    virtual = None
    for n, chunk in enumerate(chunks):
        at = slice(chunk.start, chunk.stop)
        pltpu.make_async_copy(dec.at[at], dec.at[at], dec_sem.at[n]).wait()
        pltpu.make_async_copy(enc.at[at], enc.at[at], enc_sem.at[n]).wait()
        term = lax.dot_general(
            dec[at, :KE].reshape(len(chunk) * KE, UF_DEV),
            enc[at, :KE].reshape(len(chunk) * KE, DACT * BLOCK),
            DIMS,
            preferred_element_type=jnp.float32,
        )
        virtual = term if virtual is None else virtual + term
    return virtual


def places():
    y, xl = lax.axis_index("y"), lax.axis_index("xl")
    return [
        (xl if slot % 2 == 0 else 1 - xl) * NY + lax.rem(y + TURNS[slot // 2] + NY, NY)
        for slot in range(2 * NY)
    ]


def half_kernel(*refs):
    shards, refs = refs[: 2 * NY - 1], refs[2 * NY - 1 :]
    source, virtual_ref, dec, enc, dec_sem, enc_sem = refs
    core = lax.axis_index("c")
    items = [(shard, k, core, source) for shard, k in zip(shards, places())]
    virtual_ref[...] = accumulate(items, False, dec, enc, dec_sem, enc_sem)


def score_kernel(up_ref, down_ref, *refs):
    shards, refs = refs[: 2 * NY], refs[2 * NY :]
    own, swapped, virtual_in, out_ref = refs[:4]
    dec, enc, dec_sem, enc_sem, virtual, grad, zero, scored = refs[4:12]
    in_sem, zero_sem, out_sem = refs[12:]
    zero[...] = jnp.zeros_like(zero)

    def blank(b):
        return pltpu.make_async_copy(
            zero, out_ref.at[:, b * BLOCK : (b + 1) * BLOCK], zero_sem.at[b]
        )

    idle = []
    for b in range(VF_DEV // BLOCK):
        used = down_ref[0] == b
        for i in range(1, DACT):
            used = used | (down_ref[i] == b)
        idle.append(jnp.logical_not(used))
    loads = [
        pltpu.make_async_copy(virtual_in, virtual, in_sem.at[0]),
        pltpu.make_async_copy(own.at[:, KE:], grad, in_sem.at[1]),
    ]
    for copy in loads:
        copy.start()
    core, ks = lax.axis_index("c"), places()
    items = [(shard, k, 1 - core, swapped) for shard, k in zip(shards, ks)]
    items.append((shards[-1], ks[-1], core, own))
    more = accumulate(items, True, dec, enc, dec_sem, enc_sem)
    for b in range(VF_DEV // BLOCK):
        pl.when(idle[b])(blank(b).start)
    for copy in loads:
        copy.wait()
    lane_block = lax.broadcasted_iota(jnp.int32, (TD, UF_DEV), 1) // BLOCK
    masked, kept = [], []
    for slot, k in enumerate(ks):
        on = (lane_block == up_ref[0, k // 2]) | (lane_block == up_ref[1, k // 2])
        masked.append(jnp.where(on, dec[slot, KE:].astype(jnp.float32), 0.0))
        mine, theirs = grad[k].astype(jnp.float32), enc[slot, KE:].astype(jnp.float32)
        kept += [jnp.where(core == 0, mine, theirs), jnp.where(core == 0, theirs, mine)]
    masked, kept = (jnp.concatenate(v, 0).astype(jnp.bfloat16) for v in (masked, kept))
    product = lax.dot_general(masked, kept, DIMS, preferred_element_type=jnp.float32)
    filled = []
    for i in range(DACT):
        at = slice(i * BLOCK, (i + 1) * BLOCK)
        scored[i] = product[:, at] * (virtual[:, at] + more[:, at])
        where = pl.ds(pl.multiple_of(down_ref[i] * BLOCK, BLOCK), BLOCK)
        filled.append(
            pltpu.make_async_copy(scored.at[i], out_ref.at[:, where], out_sem.at[i])
        )
        filled[i].start()
    for b in range(VF_DEV // BLOCK):
        pl.when(idle[b])(blank(b).wait)
    for copy in filled:
        copy.wait()


COLS = DACT * BLOCK


def held(count, tokens, grads):
    return [
        pltpu.VMEM((count, KE + tokens, UF_DEV), jnp.bfloat16),
        pltpu.VMEM((count, KE + grads, COLS), jnp.bfloat16),
        pltpu.SemaphoreType.DMA((-(-count // STEP),)),
        pltpu.SemaphoreType.DMA((-(-count // STEP),)),
    ]


COST = pl.CostEstimate(
    flops=UF_DEV * COLS * KD * 2 * NY, bytes_accessed=8 << 20, transcendentals=0
)


def half(shards, source):
    return pl.pallas_call(
        half_kernel,
        out_shape=jax.ShapeDtypeStruct((UF_DEV, COLS), jnp.float32),
        in_specs=[ANY] * (2 * NY),
        out_specs=VMEM,
        scratch_shapes=held(2 * NY - 1, 0, 0),
        compiler_params=pltpu.CompilerParams(vmem_limit_bytes=60 << 20),
        cost_estimate=COST,
    )(*shards, source)


def score(up_t, down_blocks, shards, own, swapped, total):
    return pl.pallas_call(
        score_kernel,
        out_shape=jax.ShapeDtypeStruct((UF_DEV, VF_DEV), jnp.float32),
        in_specs=[SMEM, SMEM] + [ANY] * (2 * NY + 3),
        out_specs=ANY,
        scratch_shapes=[
            *held(2 * NY + 1, TD, TE),
            pltpu.VMEM((UF_DEV, COLS), jnp.float32),
            pltpu.VMEM((2 * NY, TE, COLS), jnp.bfloat16),
            pltpu.VMEM((UF_DEV, BLOCK), jnp.float32),
            pltpu.VMEM((DACT, UF_DEV, BLOCK), jnp.float32),
            pltpu.SemaphoreType.DMA((2,)),
            pltpu.SemaphoreType.DMA((VF_DEV // BLOCK,)),
            pltpu.SemaphoreType.DMA((DACT,)),
        ],
        compiler_params=pltpu.CompilerParams(vmem_limit_bytes=60 << 20),
        cost_estimate=COST,
    )(up_t, down_blocks, *shards, own, swapped, total)


def turn(value, axis, by):
    n = lax.axis_size(axis)
    return lax.ppermute(value, axis, [(i, (i + by) % n) for i in range(n)])


def step(right, left):
    return turn(right, "y", 1), turn(left, "y", -1)


def local(deltas, gradients, up_blocks, down_blocks, decoder, encoder):
    d, e = pack(down_blocks, decoder.T, deltas, encoder, gradients)
    own = lax.all_to_all(e, ("z", "xh"), 0, 0, tiled=True)
    a1 = step(d, d)
    b0 = turn(d, "xl", 1)
    a2 = step(*a1)
    a3 = step(*a2)
    b1 = step(b0, b0)
    b2 = step(*b1)
    b3 = step(*b2)
    a4 = turn(a3[0], "y", 1)
    b4 = turn(a4, "xl", 1)
    own, a3, a4, b3, b4 = lax.optimization_barrier((own, a3, a4, b3, b4))
    near, across = [d, *a1, *a2, *a3, a4], [b0, *b1, *b2, *b3, b4]
    shards = [shard for both in zip(near, across) for shard in both]
    swapped = turn(own, "c", 1)
    up_t = up_blocks.T
    total = half(shards[:-1], own)
    return score(up_t, down_blocks, shards, own, swapped, total)


def solution(mesh):
    torus = Mesh(mesh.devices.reshape(8, 2, 2, 2, 8), ("z", "xh", "c", "xl", "y"))
    return jax.shard_map(
        local,
        mesh=torus,
        in_specs=(P(DOWN, UP), P(UP, DOWN), P(None, UP), P(DOWN), P(UP, DOWN), P(UP, DOWN)),
        out_specs=P(UP, DOWN),
        check_vma=False,
    )
```

```python
import jax
import jax.numpy as jnp
from jax import lax
from jax.experimental import pallas as pl
from jax.experimental.pallas import tpu as pltpu
from jax.sharding import Mesh
from jax.sharding import PartitionSpec as P

UF_DEV = 512
VF_DEV = 1024
BLOCK = 128
DACT = 4
UACT = 2
KD = 288
KE = 144
TD = 16
TE = 8
RD = KD + TD
RE = KE + TE
DOWN = ("xl", "y")
UP = ("z", "xh", "c")
NY = 8
TURNS = (0, -1, 1, -2, 2, -3, 3, 4)
STEP = 4
DIMS = (((0,), (0,)), ((), ()))
VMEM = pl.BlockSpec(memory_space=pltpu.VMEM)
SMEM = pl.BlockSpec(memory_space=pltpu.SMEM)
ANY = pl.BlockSpec(memory_space=pl.ANY)


def pack_kernel(down_ref, dec_ref, delta_ref, enc_ref, grad_ref, d_ref, e_ref, active, sems):
    copies = []

    def move(source, target):
        copies.append(pltpu.make_async_copy(source, target, sems.at[len(copies)]))
        copies[-1].start()

    for i in range(DACT):
        cols = pl.ds(pl.multiple_of(down_ref[i] * BLOCK, BLOCK), BLOCK)
        move(enc_ref.at[:, cols], active.at[:KE, i * BLOCK : (i + 1) * BLOCK])
        move(grad_ref.at[:, cols], active.at[KE:, i * BLOCK : (i + 1) * BLOCK])
    loads = len(copies)
    move(dec_ref, d_ref.at[:KD])
    move(delta_ref, d_ref.at[KD:])
    for copy in copies[:loads]:
        copy.wait()
    for n in range(2 * NY):
        move(active, e_ref.at[n])
    for copy in copies[loads:]:
        copy.wait()


def pack(down_blocks, dec_t, deltas, encoder, gradients):
    return pl.pallas_call(
        pack_kernel,
        out_shape=(
            jax.ShapeDtypeStruct((RD, UF_DEV), jnp.bfloat16),
            jax.ShapeDtypeStruct((2 * NY, RE, DACT * BLOCK), jnp.bfloat16),
        ),
        in_specs=[SMEM, ANY, ANY, ANY, ANY],
        out_specs=(VMEM, ANY),
        scratch_shapes=[
            pltpu.VMEM((RE, DACT * BLOCK), jnp.bfloat16),
            pltpu.SemaphoreType.DMA((2 * DACT + 2 + 2 * NY,)),
        ],
        compiler_params=pltpu.CompilerParams(vmem_limit_bytes=60 << 20),
    )(down_blocks, dec_t, deltas, encoder, gradients)


def accumulate(items, tokens, dec, enc, dec_sem, enc_sem, meanwhile=None):
    chunks = [range(low, min(low + STEP, len(items))) for low in range(0, len(items), STEP)]
    if len(chunks[-1]) == 1:
        chunks[-2:] = [range(chunks[-2].start, len(items))]
    for n, chunk in enumerate(chunks):
        for slot in chunk:
            shard, k, part, source = items[slot]
            rows = pl.ds(pl.multiple_of(part * KE, 16), KE)
            here = dec.at[slot]
            pltpu.make_async_copy(
                source.at[k, : enc.shape[1]], enc.at[slot], enc_sem.at[n]
            ).start()
            pltpu.make_async_copy(shard.at[rows], here.at[:KE], dec_sem.at[n]).start()
            if tokens:
                pltpu.make_async_copy(shard.at[KD:], here.at[KE:], dec_sem.at[n]).start()
    if meanwhile is not None:
        meanwhile()
    virtual = None
    for n, chunk in enumerate(chunks):
        at = slice(chunk.start, chunk.stop)
        pltpu.make_async_copy(dec.at[at], dec.at[at], dec_sem.at[n]).wait()
        pltpu.make_async_copy(enc.at[at], enc.at[at], enc_sem.at[n]).wait()
        term = lax.dot_general(
            dec[at, :KE].reshape(len(chunk) * KE, UF_DEV),
            enc[at, :KE].reshape(len(chunk) * KE, DACT * BLOCK),
            DIMS,
            preferred_element_type=jnp.float32,
        )
        virtual = term if virtual is None else virtual + term
    return virtual


def places():
    y, xl = lax.axis_index("y"), lax.axis_index("xl")
    return [
        (xl if slot % 2 == 0 else 1 - xl) * NY + lax.rem(y + TURNS[slot // 2] + NY, NY)
        for slot in range(2 * NY)
    ]


def half_kernel(*refs):
    shards, refs = refs[: 2 * NY - 1], refs[2 * NY - 1 :]
    source, virtual_ref, dec, enc, dec_sem, enc_sem = refs
    core = lax.axis_index("c")
    items = [(shard, k, core, source) for shard, k in zip(shards, places())]
    virtual_ref[...] = accumulate(items, False, dec, enc, dec_sem, enc_sem)


def score_kernel(up_ref, down_ref, *refs):
    shards, refs = refs[: 2 * NY], refs[2 * NY :]
    own, swapped, virtual_in, out_ref = refs[:4]
    dec, enc, dec_sem, enc_sem, virtual, grad, zero, scored = refs[4:12]
    in_sem, zero_sem, out_sem = refs[12:]
    zero[...] = jnp.zeros_like(zero)

    def blank(b):
        return pltpu.make_async_copy(
            zero, out_ref.at[:, b * BLOCK : (b + 1) * BLOCK], zero_sem.at[b]
        )

    idle = []
    for b in range(VF_DEV // BLOCK):
        used = down_ref[0] == b
        for i in range(1, DACT):
            used = used | (down_ref[i] == b)
        idle.append(jnp.logical_not(used))
    loads = [
        pltpu.make_async_copy(virtual_in, virtual, in_sem.at[0]),
        pltpu.make_async_copy(own.at[:, KE:], grad, in_sem.at[1]),
    ]
    for copy in loads:
        copy.start()
    core, ks = lax.axis_index("c"), places()
    items = [(shard, k, 1 - core, swapped) for shard, k in zip(shards, ks)]
    items.append((shards[-1], ks[-1], core, own))

    def blanks():
        for b in range(VF_DEV // BLOCK):
            pl.when(idle[b])(blank(b).start)

    more = accumulate(items, True, dec, enc, dec_sem, enc_sem, blanks)
    for copy in loads:
        copy.wait()
    lane_block = lax.broadcasted_iota(jnp.int32, (TD, UF_DEV), 1) // BLOCK
    masked, kept = [], []
    for slot, k in enumerate(ks):
        on = (lane_block == up_ref[0, k // 2]) | (lane_block == up_ref[1, k // 2])
        masked.append(jnp.where(on, dec[slot, KE:].astype(jnp.float32), 0.0))
        mine, theirs = grad[k].astype(jnp.float32), enc[slot, KE:].astype(jnp.float32)
        kept += [jnp.where(core == 0, mine, theirs), jnp.where(core == 0, theirs, mine)]
    masked, kept = (jnp.concatenate(v, 0).astype(jnp.bfloat16) for v in (masked, kept))
    product = lax.dot_general(masked, kept, DIMS, preferred_element_type=jnp.float32)
    filled = []
    for i in range(DACT):
        at = slice(i * BLOCK, (i + 1) * BLOCK)
        scored[i] = product[:, at] * (virtual[:, at] + more[:, at])
        where = pl.ds(pl.multiple_of(down_ref[i] * BLOCK, BLOCK), BLOCK)
        filled.append(
            pltpu.make_async_copy(scored.at[i], out_ref.at[:, where], out_sem.at[i])
        )
        filled[i].start()
    for b in range(VF_DEV // BLOCK):
        pl.when(idle[b])(blank(b).wait)
    for copy in filled:
        copy.wait()


COLS = DACT * BLOCK


def held(count, tokens, grads):
    return [
        pltpu.VMEM((count, KE + tokens, UF_DEV), jnp.bfloat16),
        pltpu.VMEM((count, KE + grads, COLS), jnp.bfloat16),
        pltpu.SemaphoreType.DMA((-(-count // STEP),)),
        pltpu.SemaphoreType.DMA((-(-count // STEP),)),
    ]


COST = pl.CostEstimate(
    flops=UF_DEV * COLS * KD * 2 * NY, bytes_accessed=8 << 20, transcendentals=0
)


def half(shards, source):
    return pl.pallas_call(
        half_kernel,
        out_shape=jax.ShapeDtypeStruct((UF_DEV, COLS), jnp.float32),
        in_specs=[ANY] * (2 * NY),
        out_specs=VMEM,
        scratch_shapes=held(2 * NY - 1, 0, 0),
        compiler_params=pltpu.CompilerParams(vmem_limit_bytes=60 << 20),
        cost_estimate=COST,
    )(*shards, source)


def score(up_t, down_blocks, shards, own, swapped, total):
    return pl.pallas_call(
        score_kernel,
        out_shape=jax.ShapeDtypeStruct((UF_DEV, VF_DEV), jnp.float32),
        in_specs=[SMEM, SMEM] + [ANY] * (2 * NY + 3),
        out_specs=ANY,
        scratch_shapes=[
            *held(2 * NY + 1, TD, TE),
            pltpu.VMEM((UF_DEV, COLS), jnp.float32),
            pltpu.VMEM((2 * NY, TE, COLS), jnp.bfloat16),
            pltpu.VMEM((UF_DEV, BLOCK), jnp.float32),
            pltpu.VMEM((DACT, UF_DEV, BLOCK), jnp.float32),
            pltpu.SemaphoreType.DMA((2,)),
            pltpu.SemaphoreType.DMA((VF_DEV // BLOCK,)),
            pltpu.SemaphoreType.DMA((DACT,)),
        ],
        compiler_params=pltpu.CompilerParams(vmem_limit_bytes=60 << 20),
        cost_estimate=COST,
    )(up_t, down_blocks, *shards, own, swapped, total)


def turn(value, axis, by):
    n = lax.axis_size(axis)
    return lax.ppermute(value, axis, [(i, (i + by) % n) for i in range(n)])


def step(right, left):
    return turn(right, "y", 1), turn(left, "y", -1)


def local(deltas, gradients, up_blocks, down_blocks, decoder, encoder):
    d, e = pack(down_blocks, decoder.T, deltas, encoder, gradients)
    own = lax.all_to_all(e, ("z", "xh"), 0, 0, tiled=True)
    a1 = step(d, d)
    b0 = turn(d, "xl", 1)
    a2 = step(*a1)
    a3 = step(*a2)
    b1 = step(b0, b0)
    b2 = step(*b1)
    b3 = step(*b2)
    a4 = turn(a3[0], "y", 1)
    b4 = turn(a4, "xl", 1)
    own, a3, a4, b3, b4 = lax.optimization_barrier((own, a3, a4, b3, b4))
    near, across = [d, *a1, *a2, *a3, a4], [b0, *b1, *b2, *b3, b4]
    shards = [shard for both in zip(near, across) for shard in both]
    swapped = turn(own, "c", 1)
    up_t = up_blocks.T
    total = half(shards[:-1], own)
    return score(up_t, down_blocks, shards, own, swapped, total)


def solution(mesh):
    torus = Mesh(mesh.devices.reshape(8, 2, 2, 2, 8), ("z", "xh", "c", "xl", "y"))
    return jax.shard_map(
        local,
        mesh=torus,
        in_specs=(P(DOWN, UP), P(UP, DOWN), P(None, UP), P(DOWN), P(UP, DOWN), P(UP, DOWN)),
        out_specs=P(UP, DOWN),
        check_vma=False,
    )
```

```python
import jax
import jax.numpy as jnp
from jax import lax
from jax.experimental import pallas as pl
from jax.experimental.pallas import tpu as pltpu
from jax.sharding import Mesh
from jax.sharding import PartitionSpec as P

UF_DEV = 512
VF_DEV = 1024
BLOCK = 128
DACT = 4
UACT = 2
KD = 288
KE = 144
TD = 16
TE = 8
RD = KD + TD
RE = KE + TE
DOWN = ("xl", "y")
UP = ("z", "xh", "c")
NY = 8
TURNS = (0, -1, 1, -2, 2, -3, 3, 4)
STEP = 5
DIMS = (((0,), (0,)), ((), ()))
VMEM = pl.BlockSpec(memory_space=pltpu.VMEM)
SMEM = pl.BlockSpec(memory_space=pltpu.SMEM)
ANY = pl.BlockSpec(memory_space=pl.ANY)


def pack_kernel(down_ref, dec_ref, delta_ref, enc_ref, grad_ref, d_ref, e_ref, active, sems):
    copies = []

    def move(source, target):
        copies.append(pltpu.make_async_copy(source, target, sems.at[len(copies)]))
        copies[-1].start()

    for i in range(DACT):
        cols = pl.ds(pl.multiple_of(down_ref[i] * BLOCK, BLOCK), BLOCK)
        move(enc_ref.at[:, cols], active.at[:KE, i * BLOCK : (i + 1) * BLOCK])
        move(grad_ref.at[:, cols], active.at[KE:, i * BLOCK : (i + 1) * BLOCK])
    loads = len(copies)
    move(dec_ref, d_ref.at[:KD])
    move(delta_ref, d_ref.at[KD:])
    for copy in copies[:loads]:
        copy.wait()
    for n in range(2 * NY):
        move(active, e_ref.at[n])
    for copy in copies[loads:]:
        copy.wait()


def pack(down_blocks, dec_t, deltas, encoder, gradients):
    return pl.pallas_call(
        pack_kernel,
        out_shape=(
            jax.ShapeDtypeStruct((RD, UF_DEV), jnp.bfloat16),
            jax.ShapeDtypeStruct((2 * NY, RE, DACT * BLOCK), jnp.bfloat16),
        ),
        in_specs=[SMEM, ANY, ANY, ANY, ANY],
        out_specs=(VMEM, ANY),
        scratch_shapes=[
            pltpu.VMEM((RE, DACT * BLOCK), jnp.bfloat16),
            pltpu.SemaphoreType.DMA((2 * DACT + 2 + 2 * NY,)),
        ],
        compiler_params=pltpu.CompilerParams(vmem_limit_bytes=60 << 20),
    )(down_blocks, dec_t, deltas, encoder, gradients)


def accumulate(items, tokens, dec, enc, dec_sem, enc_sem):
    chunks = [range(low, min(low + STEP, len(items))) for low in range(0, len(items), STEP)]
    if len(chunks[-1]) == 1:
        chunks[-2:] = [range(chunks[-2].start, len(items))]
    for n, chunk in enumerate(chunks):
        for slot in chunk:
            shard, k, part, source = items[slot]
            rows = pl.ds(pl.multiple_of(part * KE, 16), KE)
            here = dec.at[slot]
            pltpu.make_async_copy(
                source.at[k, : enc.shape[1]], enc.at[slot], enc_sem.at[n]
            ).start()
            pltpu.make_async_copy(shard.at[rows], here.at[:KE], dec_sem.at[n]).start()
            if tokens:
                pltpu.make_async_copy(shard.at[KD:], here.at[KE:], dec_sem.at[n]).start()
    virtual = None
    for n, chunk in enumerate(chunks):
        at = slice(chunk.start, chunk.stop)
        pltpu.make_async_copy(dec.at[at], dec.at[at], dec_sem.at[n]).wait()
        pltpu.make_async_copy(enc.at[at], enc.at[at], enc_sem.at[n]).wait()
        term = lax.dot_general(
            dec[at, :KE].reshape(len(chunk) * KE, UF_DEV),
            enc[at, :KE].reshape(len(chunk) * KE, DACT * BLOCK),
            DIMS,
            preferred_element_type=jnp.float32,
        )
        virtual = term if virtual is None else virtual + term
    return virtual


def places():
    y, xl = lax.axis_index("y"), lax.axis_index("xl")
    return [
        (xl if slot % 2 == 0 else 1 - xl) * NY + lax.rem(y + TURNS[slot // 2] + NY, NY)
        for slot in range(2 * NY)
    ]


def half_kernel(*refs):
    shards, refs = refs[: 2 * NY - 1], refs[2 * NY - 1 :]
    source, virtual_ref, dec, enc, dec_sem, enc_sem = refs
    core = lax.axis_index("c")
    items = [(shard, k, core, source) for shard, k in zip(shards, places())]
    virtual_ref[...] = accumulate(items, False, dec, enc, dec_sem, enc_sem)


def score_kernel(up_ref, down_ref, *refs):
    shards, refs = refs[: 2 * NY], refs[2 * NY :]
    own, swapped, virtual_in, out_ref = refs[:4]
    dec, enc, dec_sem, enc_sem, virtual, grad, zero, scored = refs[4:12]
    in_sem, zero_sem, out_sem = refs[12:]
    zero[...] = jnp.zeros_like(zero)

    def blank(b):
        return pltpu.make_async_copy(
            zero, out_ref.at[:, b * BLOCK : (b + 1) * BLOCK], zero_sem.at[b]
        )

    idle = []
    for b in range(VF_DEV // BLOCK):
        used = down_ref[0] == b
        for i in range(1, DACT):
            used = used | (down_ref[i] == b)
        idle.append(jnp.logical_not(used))
    loads = [
        pltpu.make_async_copy(virtual_in, virtual, in_sem.at[0]),
        pltpu.make_async_copy(own.at[:, KE:], grad, in_sem.at[1]),
    ]
    for copy in loads:
        copy.start()
    core, ks = lax.axis_index("c"), places()
    items = [(shard, k, 1 - core, swapped) for shard, k in zip(shards, ks)]
    items.append((shards[-1], ks[-1], core, own))
    more = accumulate(items, True, dec, enc, dec_sem, enc_sem)
    for b in range(VF_DEV // BLOCK):
        pl.when(idle[b])(blank(b).start)
    for copy in loads:
        copy.wait()
    lane_block = lax.broadcasted_iota(jnp.int32, (TD, UF_DEV), 1) // BLOCK
    masked, kept = [], []
    for slot, k in enumerate(ks):
        on = (lane_block == up_ref[0, k // 2]) | (lane_block == up_ref[1, k // 2])
        masked.append(jnp.where(on, dec[slot, KE:].astype(jnp.float32), 0.0))
        mine, theirs = grad[k].astype(jnp.float32), enc[slot, KE:].astype(jnp.float32)
        kept += [jnp.where(core == 0, mine, theirs), jnp.where(core == 0, theirs, mine)]
    masked, kept = (jnp.concatenate(v, 0).astype(jnp.bfloat16) for v in (masked, kept))
    product = lax.dot_general(masked, kept, DIMS, preferred_element_type=jnp.float32)
    filled = []
    for i in range(DACT):
        at = slice(i * BLOCK, (i + 1) * BLOCK)
        scored[i] = product[:, at] * (virtual[:, at] + more[:, at])
        where = pl.ds(pl.multiple_of(down_ref[i] * BLOCK, BLOCK), BLOCK)
        filled.append(
            pltpu.make_async_copy(scored.at[i], out_ref.at[:, where], out_sem.at[i])
        )
        filled[i].start()
    for b in range(VF_DEV // BLOCK):
        pl.when(idle[b])(blank(b).wait)
    for copy in filled:
        copy.wait()


COLS = DACT * BLOCK


def held(count, tokens, grads):
    return [
        pltpu.VMEM((count, KE + tokens, UF_DEV), jnp.bfloat16),
        pltpu.VMEM((count, KE + grads, COLS), jnp.bfloat16),
        pltpu.SemaphoreType.DMA((-(-count // STEP),)),
        pltpu.SemaphoreType.DMA((-(-count // STEP),)),
    ]


COST = pl.CostEstimate(
    flops=UF_DEV * COLS * KD * 2 * NY, bytes_accessed=8 << 20, transcendentals=0
)


def half(shards, source):
    return pl.pallas_call(
        half_kernel,
        out_shape=jax.ShapeDtypeStruct((UF_DEV, COLS), jnp.float32),
        in_specs=[ANY] * (2 * NY),
        out_specs=VMEM,
        scratch_shapes=held(2 * NY - 1, 0, 0),
        compiler_params=pltpu.CompilerParams(vmem_limit_bytes=60 << 20),
        cost_estimate=COST,
    )(*shards, source)


def score(up_t, down_blocks, shards, own, swapped, total):
    return pl.pallas_call(
        score_kernel,
        out_shape=jax.ShapeDtypeStruct((UF_DEV, VF_DEV), jnp.float32),
        in_specs=[SMEM, SMEM] + [ANY] * (2 * NY + 3),
        out_specs=ANY,
        scratch_shapes=[
            *held(2 * NY + 1, TD, TE),
            pltpu.VMEM((UF_DEV, COLS), jnp.float32),
            pltpu.VMEM((2 * NY, TE, COLS), jnp.bfloat16),
            pltpu.VMEM((UF_DEV, BLOCK), jnp.float32),
            pltpu.VMEM((DACT, UF_DEV, BLOCK), jnp.float32),
            pltpu.SemaphoreType.DMA((2,)),
            pltpu.SemaphoreType.DMA((VF_DEV // BLOCK,)),
            pltpu.SemaphoreType.DMA((DACT,)),
        ],
        compiler_params=pltpu.CompilerParams(vmem_limit_bytes=60 << 20),
        cost_estimate=COST,
    )(up_t, down_blocks, *shards, own, swapped, total)


def turn(value, axis, by):
    n = lax.axis_size(axis)
    return lax.ppermute(value, axis, [(i, (i + by) % n) for i in range(n)])


def step(right, left):
    return turn(right, "y", 1), turn(left, "y", -1)


def local(deltas, gradients, up_blocks, down_blocks, decoder, encoder):
    d, e = pack(down_blocks, decoder.T, deltas, encoder, gradients)
    own = lax.all_to_all(e, ("z", "xh"), 0, 0, tiled=True)
    a1 = step(d, d)
    b0 = turn(d, "xl", 1)
    a2 = step(*a1)
    a3 = step(*a2)
    b1 = step(b0, b0)
    b2 = step(*b1)
    b3 = step(*b2)
    a4 = turn(a3[0], "y", 1)
    b4 = turn(a4, "xl", 1)
    own, a3, a4, b3, b4 = lax.optimization_barrier((own, a3, a4, b3, b4))
    near, across = [d, *a1, *a2, *a3, a4], [b0, *b1, *b2, *b3, b4]
    shards = [shard for both in zip(near, across) for shard in both]
    swapped = turn(own, "c", 1)
    up_t = up_blocks.T
    total = half(shards[:-1], own)
    return score(up_t, down_blocks, shards, own, swapped, total)


def solution(mesh):
    torus = Mesh(mesh.devices.reshape(8, 2, 2, 2, 8), ("z", "xh", "c", "xl", "y"))
    return jax.shard_map(
        local,
        mesh=torus,
        in_specs=(P(DOWN, UP), P(UP, DOWN), P(None, UP), P(DOWN), P(UP, DOWN), P(UP, DOWN)),
        out_specs=P(UP, DOWN),
        check_vma=False,
    )
```
